32 devices in a mesh: tile: 4 (over x, core), blk: 8 (over z, y).
Axes of the slice: x: 2, y: 2, z: 4, core: 2. Of those that a mesh axis runs over, the one named last changes fastest.
Arguments:
- tokens: bfloat16 [32768, 384], P(('tile', 'blk')), may hold values from -52 to 52
- ln_gain: float32 [384], replicated, may hold values from 0.1 to 1.9
- route: int32 [32768, 2], P(('tile', 'blk')), may hold values from 0 to 15, all different within a row; in each aligned block of 1024 rows (0 to 1023, 1024 to 2047, ...) at most 192 rows name the same one
- gates: float32 [32768, 2], P(('tile', 'blk')), may hold values from 0.1 to 1
- w_gate: bfloat16 [16, 384, 1024], P('tile', 'blk'), may hold values from -0.3125 to 0.3125
- w_up: bfloat16 [16, 384, 1024], P('tile', 'blk'), may hold values from -0.3125 to 0.3125
- w_down: bfloat16 [16, 1024, 384], P('tile', 'blk'), may hold values from -0.1875 to 0.1875
- d_mixed: bfloat16 [32768, 384], P(('tile', 'blk')), may hold values from -6 to 6
Outputs:
- mixed: bfloat16 [32768, 384], P(('tile', 'blk'))
- grad_gates: float32 [32768, 2], P(('tile', 'blk'))
- grad_tokens: bfloat16 [32768, 384], P(('tile', 'blk'))
- grad_w_gate: float32 [16, 384, 1024], P('tile', 'blk')
- grad_w_up: float32 [16, 384, 1024], P('tile', 'blk')
- grad_w_down: float32 [16, 1024, 384], P('tile', 'blk')
The draws below stay inside these ranges and needn't reach their ends.
Inputs may be any that keep to these rules, and one draw needn't show every extreme that they name: `route`: each row names 2 different experts; within the rows of one device no expert is named more than 192 times, a bound that some block reaches.
All inputs are finite; a program needn't handle non-finite values.
Results may differ from the reference program's by a relative error of at most 0.014.
Values may be sent and summed in bfloat16 or wider, within the bound.
A program may use at most 192 MiB of HBM per device.

```python
import math
import jax
import jax.numpy as jnp
import numpy as np
from jax import lax

D = 384
HID = 1024
TOPK = 2
TOK_DEV = 1024
EXPERTS = 16
CAP = 192
TOKENS = 32768
N_TILE = 4
N_BLK = 8


def draw_tokens(key, part):
    key_cols, key_rows, key_offs, key_base = jax.random.split(key, 4)
    col_scale = jnp.exp(jax.random.uniform(key_cols, (D,), jnp.float32, 0.0, math.log(10.0)))
    row_scale = jnp.exp(jax.random.uniform(key_rows, (TOKENS, 1), jnp.float32, 0.0, math.log(10.0)))
    offsets = jnp.clip(jax.random.normal(key_offs, (D,), jnp.float32), -3.0, 3.0) * 0.5
    base_draw = jnp.clip(jax.random.normal(key_base, (TOKENS, D), jnp.float32), -5.0, 5.0)
    return ((base_draw * col_scale + offsets) * row_scale * 0.1).astype(jnp.bfloat16)


def steps_of(own_key, extent, cuts, least, top_value):
    def one(dim, parts):
        steps = jax.random.uniform(jax.random.fold_in(jax.random.fold_in(own_key, 6), dim), (parts,), jnp.float32, least / len(cuts), top_value / len(cuts))
        return jnp.repeat(jnp.exp(steps), extent[dim] // parts).reshape((-1,) + (1,) * (len(extent) - dim - 1))

    gain = one(*cuts[0])
    for cut in cuts[1:]:
        gain = gain * one(*cut)
    return gain


def routed_block(rng, own, number, rows, number_of, top, reach, skew):
    order = jax.random.permutation(rng, number_of)
    packed, usual = portions_of(number_of, rows * top, reach, skew, True), portions_of(number_of, rows * top, reach, skew, False)
    places = jnp.arange(number_of)

    def named(lengths, rotation):
        used = int((lengths > 0).sum())
        fixed = max(1, used // 4)
        moved = fixed + (places - fixed + rotation * (used - fixed)) % max(1, number_of - fixed)
        return jnp.zeros((number_of,), jnp.int32).at[order[jnp.where(places < fixed, places, moved)]].set(jnp.asarray(lengths, jnp.int32))

    lengths = jnp.where(number % 4 == 0, named(packed, number // 4), named(usual, number - number // 4 - 1))
    mixed = jax.random.permutation(jax.random.fold_in(own, 3), number_of)
    giver, receiver = mixed[0:number_of // 2 * 2:2], mixed[1:number_of // 2 * 2:2]
    margin = jnp.minimum(lengths[giver] - 1, reach - lengths[receiver]) // 2
    margin = jnp.where((giver == order[0]) | (receiver == order[0]) | (lengths[receiver] == 0), 0, jnp.maximum(margin, 0))
    moved = jax.random.randint(jax.random.fold_in(own, 4), (number_of // 2,), 0, 1 << 20) % (margin + 1)
    lengths = lengths.at[giver].add(-moved).at[receiver].add(moved)
    members = jnp.searchsorted(jnp.cumsum(lengths), jnp.arange(rows * top), side="right").astype(jnp.int32)
    listing = members.reshape(top, rows).T
    listing = listing[jax.random.permutation(jax.random.fold_in(own, 1), rows)]
    rotation = jax.random.randint(jax.random.fold_in(own, 2), (rows, 1), 0, top)
    return jnp.take_along_axis(listing, (jnp.arange(top)[None, :] + rotation) % top, axis=1)


def portions_of(count, total, limit, skew, full):
    loads = [(1 << 20) // math.isqrt(rank ** skew) + 1 for rank in range(1, count + 1)]
    largest = limit if full else min(limit, max(-(-total // count), total * loads[0] // sum(loads)))
    least = 1 if total - largest >= count - 1 else 0
    given, surplus = [largest] + [least] * (count - 1), total - largest - least * (count - 1)
    while surplus > 0:
        free = [i for i in range(1, count) if given[i] < largest] or [i for i in range(1, count) if given[i] < limit]
        whole, left = sum([loads[i] for i in free]), surplus
        for i in free:
            more = min(limit - given[i], max(1, left * loads[i] // whole), surplus)
            given[i] = given[i] + more
            surplus = surplus - more
    return np.array(given)


def noise(key, shape, scale, reach, cuts=(), held_as=jnp.bfloat16):
    values = scale * jax.random.normal(key, shape, jnp.float32)
    if cuts:
        values = values * steps_of(key, shape, cuts, -0.22, 0.18)
    return jnp.clip(values, -reach, reach).astype(held_as)


def setup_inputs(seed: int = 0) -> dict:
    streams_of = jax.random.split(jax.random.key(seed), 9)
    tokens = draw_tokens(jax.random.fold_in(streams_of[8], 71), 0)
    ln_gain = jnp.clip(1.0 + 0.18 * jax.random.normal(streams_of[1], (D,), jnp.float32), 0.1, 1.9)
    route_keys = jax.random.split(jax.random.fold_in(streams_of[2], 1), TOKENS // TOK_DEV)
    route_turns = jax.random.permutation(jax.random.fold_in(streams_of[2], 3), TOKENS // TOK_DEV)
    route = jax.vmap(lambda own, number: routed_block(jax.random.fold_in(streams_of[2], 2), own, number, TOK_DEV, EXPERTS, TOPK, CAP, 2))(route_keys, route_turns).reshape((TOKENS, TOPK))
    gates = jnp.clip(jnp.exp(math.log(1.0) - 2.3025851 * jax.random.uniform(streams_of[3], (TOKENS, TOPK), jnp.float32) ** steps_of(streams_of[3], (TOKENS, TOPK), ((0, 32),), -0.2, 0.2)), 0.1, 1.0)
    w_gate = noise(streams_of[4], (EXPERTS, D, HID), D ** -0.5, 0.3125, ((0, 4), (1, 8)))
    w_up = noise(streams_of[5], (EXPERTS, D, HID), D ** -0.5, 0.3125, ((0, 4), (1, 8)))
    w_down = noise(streams_of[6], (EXPERTS, HID, D), HID ** -0.5, 0.1875, ((0, 4), (1, 8)))
    d_mixed = noise(streams_of[7], (TOKENS, D), 1.0, 6.0, ((0, 32),))
    return dict(tokens=tokens, ln_gain=ln_gain, route=route, gates=gates, w_gate=w_gate, w_up=w_up, w_down=w_down, d_mixed=d_mixed)


def layer_norm(values, ln_gain):
    centre = lax.optimization_barrier(jnp.mean(values, axis=-1, keepdims=True))
    centred = values - centre
    spread = lax.optimization_barrier(jnp.mean(centred * centred, axis=-1, keepdims=True))
    return values * lax.rsqrt(spread + 1e-05) * ln_gain

def reference(tokens, ln_gain, route, gates, w_gate, w_up, w_down, d_mixed):
    tokens_wide = tokens.astype(jnp.float32)
    normed = layer_norm(tokens_wide, ln_gain).astype(jnp.bfloat16)
    count = TOKENS * TOPK
    most_rows = N_TILE * N_BLK * CAP
    flat_route = route.reshape(-1).astype(jnp.int32)
    owner_token = jnp.arange(count, dtype=jnp.int32) // TOPK
    onehot = (flat_route[:, None] == jnp.arange(EXPERTS, dtype=jnp.int32)[None, :]).astype(jnp.int32)
    slot_rank = lax.optimization_barrier(jnp.sum((jnp.cumsum(onehot, axis=0) - 1) * onehot, axis=1)).astype(jnp.int32)
    slot_index = (flat_route * most_rows + slot_rank).astype(jnp.int32)
    table = jnp.full((EXPERTS * most_rows,), count, jnp.int32)
    table = table.at[slot_index].set(jnp.arange(count, dtype=jnp.int32)).reshape(EXPERTS, most_rows)
    d_wide = d_mixed.astype(jnp.float32)
    d_assign = (gates.reshape(-1)[:, None] * d_wide[owner_token]).astype(jnp.bfloat16)
    normed_pad = jnp.concatenate([normed, jnp.zeros((1, D), jnp.bfloat16)], axis=0)
    d_pad = jnp.concatenate([d_assign, jnp.zeros((1, D), jnp.bfloat16)], axis=0)
    token_pad = jnp.concatenate([owner_token, jnp.full((1,), TOKENS, jnp.int32)], axis=0)

    def per_expert(inputs):
        indices, weight_gate, weight_up, weight_down = inputs
        inputs_rows = normed_pad[token_pad[indices]]
        d_rows = d_pad[indices]
        gate_pre = jnp.dot(inputs_rows, weight_gate, preferred_element_type=jnp.float32)
        up_pre = jnp.dot(inputs_rows, weight_up, preferred_element_type=jnp.float32)
        sigma_gate = jax.nn.sigmoid(gate_pre)
        hidden_act = (gate_pre * sigma_gate * up_pre).astype(jnp.bfloat16)
        expert_rows = jnp.dot(hidden_act, weight_down, preferred_element_type=jnp.float32).astype(jnp.bfloat16)
        d_act = jnp.dot(d_rows, weight_down.T, preferred_element_type=jnp.float32)
        d_gate = (d_act * up_pre * sigma_gate * (1.0 + gate_pre * (1.0 - sigma_gate))).astype(jnp.bfloat16)
        d_up = (d_act * gate_pre * sigma_gate).astype(jnp.bfloat16)
        d_in = (jnp.dot(d_gate, weight_gate.T, preferred_element_type=jnp.float32) + jnp.dot(d_up, weight_up.T, preferred_element_type=jnp.float32)).astype(jnp.bfloat16)
        grad_gate = jnp.dot(inputs_rows.T, d_gate, preferred_element_type=jnp.float32)
        grad_up = jnp.dot(inputs_rows.T, d_up, preferred_element_type=jnp.float32)
        grad_down = jnp.dot(hidden_act.T, d_rows, preferred_element_type=jnp.float32)
        return (expert_rows, d_in, grad_gate, grad_up, grad_down)
    out_rows, din_rows, grad_w_gate, grad_w_up, grad_w_down = lax.map(per_expert, (table, w_gate, w_up, w_down))
    expert_out = out_rows.reshape(-1, D)[slot_index].astype(jnp.float32).reshape(TOKENS, TOPK, D)
    mixed = lax.optimization_barrier(jnp.sum(gates[:, :, None] * expert_out, axis=1)).astype(jnp.bfloat16)
    grad_gates = lax.optimization_barrier(jnp.sum(d_wide[:, None, :] * expert_out, axis=-1))
    d_normed = lax.optimization_barrier(jnp.sum(din_rows.reshape(-1, D)[slot_index].astype(jnp.float32).reshape(TOKENS, TOPK, D), axis=1))

    def normalize(values):
        return layer_norm(values, ln_gain)
    unused, pullback = jax.vjp(normalize, tokens_wide)
    grad_tokens = pullback(d_normed)[0].astype(jnp.bfloat16)
    return (mixed, grad_gates, grad_tokens, grad_w_gate, grad_w_up, grad_w_down)
```

```python
import functools
import math

import jax
import jax.numpy as jnp
from jax import lax
from jax.experimental import pallas as pl
from jax.experimental.pallas import tpu as pltpu
from jax.sharding import PartitionSpec as P

F32 = jnp.float32
BF16 = jnp.bfloat16
MESH = pl.DeviceIdType.MESH


def ring_order(count):
    inner = max(d for d in range(1, math.isqrt(count) + 1) if count % d == 0)
    outer = count // inner
    walk = [row * inner for row in range(outer)]
    for step, row in enumerate(reversed(range(outer))):
        cols = list(range(1, inner))
        if step % 2:
            cols.reverse()
        walk += [row * inner + col for col in cols]
    return walk


def lookup(table, index):
    total = jnp.int32(0)
    for place, value in enumerate(table):
        total = total + jnp.where(index == place, jnp.int32(value), jnp.int32(0))
    return total


def matmul(left, right, dims):
    return lax.dot_general(left, right, (dims, ((), ())), preferred_element_type=F32)


def kernel(
    tiles, blks, per_tile, cap,
    tok, gain, route, route_t, gates, w_gate, w_up, w_down, dmix,
    mixed, grad_gates, grad_tok, out_gu, out_dn,
    wgu, wdn, xs, ds, xr, dr, yr, dyr, ggu, gdn, rgu, rdn, tmp, slot_c, slot_r,
    load_sem, ag_send, ag_recv, rs_send, rs_recv, go_send, go_recv, go_own,
    back_send, back_recv, back_own,
):
    rows, feats = tok.shape
    hid = w_gate.shape[2]
    experts = tiles * per_tile
    half = hid // 2
    t = lax.axis_index("tile")
    b = lax.axis_index("blk")
    walk = ring_order(blks)
    where_is = [walk.index(i) for i in range(blks)]
    pos = lookup(where_is, b)

    def at(place):
        return lookup(walk, lax.rem(place + 4 * blks, blks))

    ring = (at(pos + 1), at(pos - 1))
    signs = (1, -1)

    def peer(jj):
        return lax.rem(t + jj, tiles)

    def source(jj):
        return lax.rem(t - jj + tiles, tiles)

    loads = []
    for index, (src, dst) in enumerate(
        ((w_gate, wgu.at[:, 0, b]), (w_up, wgu.at[:, 1, b]), (w_down, wdn.at[:, b]))
    ):
        loads.append(pltpu.make_async_copy(src, dst, load_sem.at[index]))
        loads[-1].start()

    barrier = pltpu.get_barrier_semaphore()
    for place in ring:
        pl.semaphore_signal(barrier, inc=1, device_id=(t, place), device_id_type=MESH)
    for jj in range(1, tiles):
        pl.semaphore_signal(barrier, inc=1, device_id=(peer(jj), b), device_id_type=MESH)
    pl.semaphore_wait(barrier, 2 + tiles - 1)
    for load in loads:
        load.wait()

    def ag_copies(e, s, way):
        owner = at(pos - signs[way] * s)
        return [
            pltpu.make_async_remote_copy(
                src_ref=ref, dst_ref=ref,
                send_sem=ag_send.at[e, way, s, part], recv_sem=ag_recv.at[e, way, s, part],
                device_id=(t, ring[way]), device_id_type=MESH,
            )
            for part, ref in enumerate((wgu.at[e, :, owner], wdn.at[e, owner]))
        ]

    def ag_wait_copies(e, s, way):
        owner = at(pos - signs[way] * (s + 1))
        return [
            pltpu.make_async_remote_copy(
                src_ref=ref, dst_ref=ref,
                send_sem=ag_send.at[e, way, s, part], recv_sem=ag_recv.at[e, way, s, part],
                device_id=(t, ring[way]), device_id_type=MESH,
            )
            for part, ref in enumerate((wgu.at[e, :, owner], wdn.at[e, owner]))
        ]

    hops = blks // 2

    def ag_each(e, s, action):
        for way in range(2):
            @pl.when(jnp.logical_or(s < hops - 1, jnp.logical_and(s == hops - 1, lax.rem(e, 2) == way)))
            def _():
                action(e, s, way)

    def ag_start(e, s):
        def go(e, s, way):
            for copy in ag_copies(e, s, way):
                copy.start()
        ag_each(e, s, go)

    def ag_wait(e, s):
        def land(e, s, way):
            for copy in ag_wait_copies(e, s, way):
                copy.wait_recv()
        ag_each(e, s, land)

    def ag_sent(e, s):
        def done(e, s, way):
            for copy in ag_copies(e, s, way):
                copy.wait_send()
        ag_each(e, s, done)

    def rs_copies(e, s, way):
        chunk = at(pos - signs[way] * (s + 1))
        return [
            pltpu.make_async_remote_copy(
                src_ref=src, dst_ref=dst,
                send_sem=rs_send.at[e, way, s, part], recv_sem=rs_recv.at[e, way, s, part],
                device_id=(t, ring[way]), device_id_type=MESH,
            )
            for part, (src, dst) in enumerate((
                (ggu.at[e, way, chunk], rgu.at[e, way, s]),
                (gdn.at[e, way, chunk], rdn.at[e, way, s]),
            ))
        ]

    def rs_start(e, s):
        for way in range(2):
            for copy in rs_copies(e, s, way):
                copy.start()

    last = blks - 2

    def rs_step(e, s):
        for way in range(2):
            for copy in rs_copies(e, s, way):
                copy.wait_recv()
            chunk = at(pos - signs[way] * (s + 2))
            gu = ggu[e, way, chunk].astype(F32) + rgu[e, way, s].astype(F32)
            dn = gdn[e, way, chunk].astype(F32) + rdn[e, way, s].astype(F32)

            @pl.when(s < last)
            def _():
                ggu[e, way, chunk] = gu.astype(BF16)
                gdn[e, way, chunk] = dn.astype(BF16)
                for copy in rs_copies(e, s + 1, way):
                    copy.start()

            @pl.when(s == last)
            def _():
                out_gu[e, way] = gu
                out_dn[e, way] = dn

    def row_copies(src, dst, send, recv, own, e, jj, part, place):
        def here():
            return pltpu.make_async_copy(src, dst, own.at[e, part])

        def there():
            return pltpu.make_async_remote_copy(
                src_ref=src, dst_ref=dst, send_sem=send.at[e, jj, part],
                recv_sem=recv.at[e, jj, part], device_id=(place, b), device_id_type=MESH,
            )

        return here, there

    def go_pairs(e, jj, at_tile):
        return [
            row_copies(src.at[e, jj], dst.at[e, at_tile], go_send, go_recv, go_own, e, jj, part, peer(jj))
            for part, (src, dst) in enumerate(((xs, xr), (ds, dr)))
        ]

    def back_pairs(e, jj, at_tile):
        return [
            row_copies(src.at[e, peer(jj)], dst.at[at_tile, e], back_send, back_recv, back_own, e, jj, part, peer(jj))
            for part, (src, dst) in enumerate(((xr, yr), (dr, dyr)))
        ]

    for e in range(min(2, per_tile)):
        ag_start(e, 0)

    block = min(256, rows)

    def slots(i, carry):
        base = pl.multiple_of(i * block, block)
        names = lax.broadcasted_iota(jnp.int32, (rows, experts), 1)
        count = (route[:, 0:1] == names).astype(F32) + (route[:, 1:2] == names).astype(F32)
        row = lax.broadcasted_iota(jnp.int32, (block, rows), 0) + base
        col = lax.broadcasted_iota(jnp.int32, (block, rows), 1)
        before = matmul((col < row).astype(F32).astype(BF16), count.astype(BF16), ((1,), (0,)))
        part = route[pl.ds(base, block), :]
        name = lax.broadcasted_iota(jnp.int32, (block, experts), 1)
        for k in range(2):
            mine = part[:, k : k + 1]
            rank = jnp.sum(jnp.where(mine == name, before, 0.0), axis=1, keepdims=True)
            slot_c[pl.ds(base, block), k : k + 1] = mine * cap + rank.astype(jnp.int32)
        names_t = lax.broadcasted_iota(jnp.int32, (experts, rows), 0)
        count_t = (route_t[0:1, :] == names_t).astype(F32) + (route_t[1:2, :] == names_t).astype(F32)
        row_t = lax.broadcasted_iota(jnp.int32, (rows, block), 0)
        col_t = lax.broadcasted_iota(jnp.int32, (rows, block), 1) + base
        before_t = matmul(count_t.astype(BF16), (row_t < col_t).astype(F32).astype(BF16), ((1,), (0,)))
        part_t = route_t[:, pl.ds(base, block)]
        name_t = lax.broadcasted_iota(jnp.int32, (experts, block), 0)
        for k in range(2):
            mine = part_t[k : k + 1, :]
            rank = jnp.sum(jnp.where(mine == name_t, before_t, 0.0), axis=0, keepdims=True)
            slot_r[k : k + 1, pl.ds(base, block)] = mine * cap + rank.astype(jnp.int32)
        x = tok[pl.ds(base, block), :].astype(F32)
        centred = x - jnp.mean(x, axis=-1, keepdims=True)
        spread = jnp.mean(centred * centred, axis=-1, keepdims=True)
        d = dmix[pl.ds(base, block), :].astype(F32)
        g = gates[pl.ds(base, block), :]
        tmp[0, pl.ds(base, block), 0:feats] = (x * lax.rsqrt(spread + 1e-05) * gain[...]).astype(BF16)
        tmp[1, pl.ds(base, block), 0:feats] = (g[:, 0:1] * d).astype(BF16)
        tmp[2, pl.ds(base, block), 0:feats] = (g[:, 1:2] * d).astype(BF16)
        return carry

    lax.fori_loop(0, rows // block, slots, 0)

    def pack(i, carry):
        e, jj = i // tiles, lax.rem(i, tiles)
        dest = peer(jj)
        want = lax.broadcasted_iota(jnp.int32, (cap, rows), 0) + (dest * per_tile + e) * cap
        first = (slot_r[0:1, :] == want).astype(F32)
        second = (slot_r[1:2, :] == want).astype(F32)
        xs[e, jj] = matmul((first + second).astype(BF16), tmp[0, 0:rows, 0:feats], ((1,), (0,))).astype(BF16)
        ds[e, jj] = (
            matmul(first.astype(BF16), tmp[1, 0:rows, 0:feats], ((1,), (0,)))
            + matmul(second.astype(BF16), tmp[2, 0:rows, 0:feats], ((1,), (0,)))
        ).astype(BF16)

        @pl.when(jj == 0)
        def _():
            for here, there in go_pairs(e, jj, t):
                here().start()

        @pl.when(jj > 0)
        def _():
            for here, there in go_pairs(e, jj, t):
                there().start()

        return carry

    lax.fori_loop(0, per_tile * tiles, pack, 0)

    for s in range(hops):
        for e in range(min(2, per_tile)):
            ag_wait(e, s)
            if s + 1 < hops:
                ag_start(e, s + 1)

    def service(e, k):
        @pl.when(jnp.logical_and(e + 2 < per_tile, k < hops))
        def _():
            ag_wait(e + 2, k)

            @pl.when(k + 1 < hops)
            def _():
                ag_start(e + 2, k + 1)

        @pl.when(jnp.logical_and(e >= 1, k <= last))
        def _():
            rs_step(e - 1, k)

    def expert(e, carry):
        @pl.when(e + 2 < per_tile)
        def _():
            ag_start(e + 2, 0)

        for jj in range(tiles):
            for here, there in go_pairs(e, jj, source(jj)):
                if jj == 0:
                    here().wait()
                else:
                    there().wait_recv()

        def forward(i, carry):
            span = pl.ds(pl.multiple_of(i * cap, cap), cap)
            x, d = xr[e, i], dr[e, i]
            wide = (feats, hid)
            gate_pre = matmul(x, wgu[e, 0].reshape(wide), ((1,), (0,)))
            up_pre = matmul(x, wgu[e, 1].reshape(wide), ((1,), (0,)))
            d_act = matmul(d, wdn[e].reshape(hid, feats), ((1,), (1,)))
            sigma = jax.nn.sigmoid(gate_pre)
            swish = gate_pre * sigma
            tmp[0, span, :] = (swish * up_pre).astype(BF16)
            tmp[1, span, :] = (d_act * up_pre * sigma * (1.0 + gate_pre * (1.0 - sigma))).astype(BF16)
            tmp[2, span, :] = (d_act * swish).astype(BF16)
            service(e, i)
            return carry

        lax.fori_loop(0, tiles, forward, 0)

        many = tiles * cap
        x_all = xr[e].reshape(many, feats)
        for part in range(2):
            for way in range(2):
                grad = matmul(x_all, tmp[1 + part, 0:many, way * half : (way + 1) * half], ((0,), (0,)))
                ggu[e, way, :, part] = grad.reshape(blks, feats // blks, half).astype(BF16)
        width = min(256, hid)
        deep = hid // blks

        def down(i, carry):
            span = pl.ds(pl.multiple_of(i * width, width), width)
            grad = matmul(tmp[0, 0:many, span], dr[e].reshape(many, feats), ((0,), (0,)))
            grad = grad.reshape(width // deep, 2, deep // 2, feats).astype(BF16)
            for c in range(width // deep):
                for way in range(2):
                    gdn[e, way, i * (width // deep) + c] = grad[c, way]
            return carry

        lax.fori_loop(0, hid // width, down, 0)
        rs_start(e, 0)

        def backward(i, carry):
            span = pl.ds(pl.multiple_of(i * cap, cap), cap)
            wide = (feats, hid)
            y = matmul(tmp[0, span, :], wdn[e].reshape(hid, feats), ((1,), (0,)))
            d_in = matmul(tmp[1, span, :], wgu[e, 0].reshape(wide), ((1,), (1,)))
            d_in = d_in + matmul(tmp[2, span, :], wgu[e, 1].reshape(wide), ((1,), (1,)))
            xr[e, i] = y.astype(BF16)
            dr[e, i] = d_in.astype(BF16)
            service(e, tiles + i)
            return carry

        lax.fori_loop(0, tiles, backward, 0)
        for jj in range(tiles):
            for here, there in back_pairs(e, jj, t):
                (there if jj else here)().start()

        def rest(i, carry):
            service(e, i)
            return carry

        lax.fori_loop(2 * tiles, max(2 * tiles, blks - 1, hops), rest, 0)
        return carry

    lax.fori_loop(0, per_tile, expert, 0)

    def returned(e, carry):
        for jj in range(tiles):
            for here, there in back_pairs(e, jj, source(jj)):
                if jj == 0:
                    here().wait()
                else:
                    there().wait_recv()
        return carry

    lax.fori_loop(0, per_tile, returned, 0)

    def finish(i):
        base = pl.multiple_of(i * block, block)
        span = pl.ds(base, block)
        every = experts * cap
        want = lax.broadcasted_iota(jnp.int32, (block, every), 1)
        first = (slot_c[span, 0:1] == want).astype(F32)
        second = (slot_c[span, 1:2] == want).astype(F32)
        y = yr[...].reshape(every, feats)
        y0 = matmul(first.astype(BF16), y, ((1,), (0,)))
        y1 = matmul(second.astype(BF16), y, ((1,), (0,)))
        dn = matmul((first + second).astype(BF16), dyr[...].reshape(every, feats), ((1,), (0,)))
        g = gates[span, :]
        d = dmix[span, :].astype(F32)
        mixed[span, :] = (g[:, 0:1] * y0 + g[:, 1:2] * y1).astype(BF16)
        grad_gates[span, 0:1] = jnp.sum(d * y0, axis=-1, keepdims=True)
        grad_gates[span, 1:2] = jnp.sum(d * y1, axis=-1, keepdims=True)
        x = tok[span, :].astype(F32)
        centred = x - jnp.mean(x, axis=-1, keepdims=True)
        spread = jnp.mean(centred * centred, axis=-1, keepdims=True)
        r = lax.rsqrt(spread + 1e-05)
        u = dn * gain[...]
        pull = jnp.sum(u * x, axis=-1, keepdims=True) * (r * r * r) / feats
        grad_tok[span, :] = (u * r - pull * centred).astype(BF16)

    def tail(s, carry):
        @pl.when(s <= last)
        def _():
            rs_step(per_tile - 1, s)

        @pl.when(s < rows // block)
        def _():
            finish(s)

        return carry

    lax.fori_loop(0, max(blks - 1, rows // block), tail, 0)

    def drain(e, carry):
        def ag_done(s, carry):
            ag_sent(e, s)
            return carry

        lax.fori_loop(0, hops, ag_done, 0)

        def rs_done(s, carry):
            for way in range(2):
                for copy in rs_copies(e, s, way):
                    copy.wait_send()
            return carry

        lax.fori_loop(0, blks - 1, rs_done, 0)
        for jj in range(1, tiles):
            for here, there in go_pairs(e, jj, t) + back_pairs(e, jj, t):
                there().wait_send()
        return carry

    lax.fori_loop(0, per_tile, drain, 0)


def on_device(tiles, blks, tokens, ln_gain, route, gates, w_gate, w_up, w_down, d_mixed):
    rows, feats = tokens.shape
    per_tile, thin, hid = w_gate.shape
    deep = w_down.shape[1]
    experts = per_tile * tiles
    cap = max(2, 3 * rows * route.shape[1] // (2 * experts))
    half = hid // 2
    hops = blks // 2
    vmem = pl.BlockSpec(memory_space=pltpu.VMEM)
    hbm = pl.BlockSpec(memory_space=pl.ANY)
    moved = (per_tile, tiles, cap, feats)
    dma = pltpu.SemaphoreType.DMA
    outs = pl.pallas_call(
        functools.partial(kernel, tiles, blks, per_tile, cap),
        out_shape=(
            jax.ShapeDtypeStruct((rows, feats), BF16),
            jax.ShapeDtypeStruct((rows, 2), F32),
            jax.ShapeDtypeStruct((rows, feats), BF16),
            jax.ShapeDtypeStruct((per_tile, 2, 2, thin, half), F32),
            jax.ShapeDtypeStruct((per_tile, 2, deep // 2, feats), F32),
        ),
        in_specs=[vmem, vmem, vmem, vmem, vmem, hbm, hbm, hbm, vmem],
        out_specs=[vmem] * 5,
        scratch_shapes=[
            pltpu.VMEM((per_tile, 2, blks, thin, hid), BF16),
            pltpu.VMEM((per_tile, blks, deep, feats), BF16),
            pltpu.VMEM(moved, BF16),
            pltpu.VMEM(moved, BF16),
            pltpu.VMEM(moved, BF16),
            pltpu.VMEM(moved, BF16),
            pltpu.VMEM((tiles, per_tile, cap, feats), BF16),
            pltpu.VMEM((tiles, per_tile, cap, feats), BF16),
            pltpu.VMEM((per_tile, 2, blks, 2, thin, half), BF16),
            pltpu.VMEM((per_tile, 2, blks, deep // 2, feats), BF16),
            pltpu.VMEM((per_tile, 2, blks - 1, 2, thin, half), BF16),
            pltpu.VMEM((per_tile, 2, blks - 1, deep // 2, feats), BF16),
            pltpu.VMEM((3, max(rows, tiles * cap), max(hid, feats)), BF16),
            pltpu.VMEM((rows, 2), jnp.int32),
            pltpu.VMEM((2, rows), jnp.int32),
            dma((3,)),
            dma((per_tile, 2, hops, 2)),
            dma((per_tile, 2, hops, 2)),
            dma((per_tile, 2, blks - 1, 2)),
            dma((per_tile, 2, blks - 1, 2)),
            dma((per_tile, tiles, 2)),
            dma((per_tile, tiles, 2)),
            dma((per_tile, 2)),
            dma((per_tile, tiles, 2)),
            dma((per_tile, tiles, 2)),
            dma((per_tile, 2)),
        ],
        compiler_params=pltpu.CompilerParams(
            collective_id=0, has_side_effects=True, vmem_limit_bytes=67043328
        ),
    )(tokens, ln_gain.reshape(1, feats), route, route.T, gates, w_gate, w_up, w_down, d_mixed)
    mixed, grad_gates, grad_tokens, gu, dn = outs
    gu = gu.transpose(2, 0, 3, 1, 4).reshape(2, per_tile, thin, hid)
    return (mixed, grad_gates, grad_tokens, gu[0], gu[1], dn.reshape(per_tile, deep, feats))


def solution(mesh):
    rows_spec = P(("tile", "blk"), None)
    weight_spec = P("tile", "blk", None)
    return jax.shard_map(
        functools.partial(on_device, mesh.shape["tile"], mesh.shape["blk"]),
        mesh=mesh,
        in_specs=(rows_spec, P(), rows_spec, rows_spec) + (weight_spec,) * 3 + (rows_spec,),
        out_specs=(rows_spec,) * 3 + (weight_spec,) * 3,
        check_vma=False,
    )
```

```python
import functools
import math

import jax
import jax.numpy as jnp
from jax import lax
from jax.experimental import pallas as pl
from jax.experimental.pallas import tpu as pltpu
from jax.sharding import PartitionSpec as P

F32 = jnp.float32
BF16 = jnp.bfloat16
MESH = pl.DeviceIdType.MESH


def ring_order(count):
    inner = max(d for d in range(1, math.isqrt(count) + 1) if count % d == 0)
    outer = count // inner
    walk = [row * inner for row in range(outer)]
    for step, row in enumerate(reversed(range(outer))):
        cols = list(range(1, inner))
        if step % 2:
            cols.reverse()
        walk += [row * inner + col for col in cols]
    return walk


def lookup(table, index):
    total = jnp.int32(0)
    for place, value in enumerate(table):
        total = total + jnp.where(index == place, jnp.int32(value), jnp.int32(0))
    return total


def matmul(left, right, dims):
    return lax.dot_general(left, right, (dims, ((), ())), preferred_element_type=F32)


class Later:
    def __init__(self, **parts):
        self.parts = parts

    def __getattr__(self, name):
        return getattr(pltpu.make_async_remote_copy(**self.parts), name)


def kernel(
    tiles, blks, per_tile, cap,
    tok, gain, route_t, gates_t, w_gate, w_up, w_down, dmix,
    mixed, grad_gates, grad_tok, out_gate, out_up, out_dn,
    wgu, wdn, xs, ds, xr, dr, yr, dyr, ggu, gdn, rgu, rdn, tmp, cols, slot_r,
    load_sem, ag_send, ag_recv, rs_send, rs_recv, go_send, go_recv, go_own,
    back_send, back_recv, back_own,
):
    rows, feats = tok.shape
    hid = w_gate.shape[2]
    experts = tiles * per_tile
    half = hid // 2
    deep = hid // blks
    t = lax.axis_index("tile")
    b = lax.axis_index("blk")
    walk = ring_order(blks)
    where_is = [walk.index(i) for i in range(blks)]
    pos = lookup(where_is, b)

    def at(place):
        return lookup(walk, lax.rem(place + 4 * blks, blks))

    ring = (at(pos + 1), at(pos - 1))
    signs = (1, -1)

    def peer(jj):
        return lax.rem(t + jj, tiles)

    def source(jj):
        return lax.rem(t - jj + tiles, tiles)

    loads = []
    for index, (src, dst) in enumerate(
        ((w_gate, wgu.at[:, 0, b]), (w_up, wgu.at[:, 1, b]), (w_down, wdn.at[:, b]))
    ):
        loads.append(pltpu.make_async_copy(src, dst, load_sem.at[index]))
        loads[-1].start()

    barrier = pltpu.get_barrier_semaphore()
    for place in ring:
        pl.semaphore_signal(barrier, inc=1, device_id=(t, place), device_id_type=MESH)
    for jj in range(1, tiles):
        pl.semaphore_signal(barrier, inc=1, device_id=(peer(jj), b), device_id_type=MESH)
    pl.semaphore_wait(barrier, 2 + tiles - 1)
    for load in loads:
        load.wait()

    def ag_copies(e, s, way):
        owner = at(pos - signs[way] * s)
        return [
            pltpu.make_async_remote_copy(
                src_ref=ref, dst_ref=ref,
                send_sem=ag_send.at[e, way, s, part], recv_sem=ag_recv.at[e, way, s, part],
                device_id=(t, ring[way]), device_id_type=MESH,
            )
            for part, ref in enumerate((wgu.at[e, :, owner], wdn.at[e, owner]))
        ]

    def ag_wait_copies(e, s, way):
        owner = at(pos - signs[way] * (s + 1))
        return [
            pltpu.make_async_remote_copy(
                src_ref=ref, dst_ref=ref,
                send_sem=ag_send.at[e, way, s, part], recv_sem=ag_recv.at[e, way, s, part],
                device_id=(t, ring[way]), device_id_type=MESH,
            )
            for part, ref in enumerate((wgu.at[e, :, owner], wdn.at[e, owner]))
        ]

    hops = blks // 2

    def ag_each(e, s, action):
        for way in range(2):
            @pl.when(jnp.logical_or(s < hops - 1, jnp.logical_and(s == hops - 1, lax.rem(e, 2) == way)))
            def _():
                action(e, s, way)

    def ag_start(e, s):
        def go(e, s, way):
            for copy in ag_copies(e, s, way):
                copy.start()
        ag_each(e, s, go)

    def ag_wait(e, s):
        def land(e, s, way):
            for copy in ag_wait_copies(e, s, way):
                copy.wait_recv()
        ag_each(e, s, land)

    def ag_sent(e, s):
        def done(e, s, way):
            for copy in ag_copies(e, s, way):
                copy.wait_send()
        ag_each(e, s, done)

    def rs_copies(e, s, way):
        chunk = at(pos - signs[way] * (s + 1))
        return [
            Later(
                src_ref=src, dst_ref=dst,
                send_sem=rs_send.at[e, way, s, part], recv_sem=rs_recv.at[e, way, s, part],
                device_id=(t, ring[way]), device_id_type=MESH,
            )
            for part, (src, dst) in enumerate((
                (ggu.at[e, way, chunk], rgu.at[e, way, s]),
                (gdn.at[e, way, chunk], rdn.at[e, way, s]),
            ))
        ]

    def rs_start(e, s):
        for way in range(2):
            for copy in rs_copies(e, s, way):
                copy.start()

    last = blks - 2

    def rs_step(e, s):
        for part, (own, landed) in enumerate(((ggu, rgu), (gdn, rdn))):
            for way in range(2):
                rs_copies(e, s, way)[part].wait_recv()
                chunk = at(pos - signs[way] * (s + 2))
                total = own[e, way, chunk].astype(F32) + landed[e, way, s].astype(F32)

                @pl.when(s < last)
                def _():
                    own[e, way, chunk] = total.astype(BF16)
                    rs_copies(e, s + 1, way)[part].start()

                @pl.when(s == last)
                def _():
                    if part:
                        out_dn[e, way * (deep // 2) : (way + 1) * (deep // 2), :] = total
                    else:
                        out_gate[e, :, way * half : (way + 1) * half] = total[0]
                        out_up[e, :, way * half : (way + 1) * half] = total[1]

    def row_copies(src, dst, send, recv, own, e, jj, part, place):
        def here():
            return pltpu.make_async_copy(src, dst, own.at[e, part])

        def there():
            return pltpu.make_async_remote_copy(
                src_ref=src, dst_ref=dst, send_sem=send.at[e, jj, part],
                recv_sem=recv.at[e, jj, part], device_id=(place, b), device_id_type=MESH,
            )

        return here, there

    def go_pairs(e, jj, at_tile):
        return [
            row_copies(src.at[e, jj], dst.at[e, at_tile], go_send, go_recv, go_own, e, jj, part, peer(jj))
            for part, (src, dst) in enumerate(((xs, xr), (ds, dr)))
        ]

    def back_pairs(e, jj, at_tile):
        return [
            row_copies(src.at[e, peer(jj)], dst.at[at_tile, e], back_send, back_recv, back_own, e, jj, part, peer(jj))
            for part, (src, dst) in enumerate(((xr, yr), (dr, dyr)))
        ]

    for e in range(min(2, per_tile)):
        ag_start(e, 0)

    block = min(256, rows)

    def slots(i, carry):
        base = pl.multiple_of(i * block, block)
        span = pl.ds(base, block)
        names = lax.broadcasted_iota(jnp.int32, (experts, rows), 0)
        count = (route_t[0:1, :] == names).astype(F32) + (route_t[1:2, :] == names).astype(F32)
        row = lax.broadcasted_iota(jnp.int32, (rows, block), 0)
        col = lax.broadcasted_iota(jnp.int32, (rows, block), 1) + base
        before = matmul(count.astype(BF16), (row < col).astype(F32).astype(BF16), ((1,), (0,)))
        part = route_t[:, span]
        name = lax.broadcasted_iota(jnp.int32, (experts, block), 0)
        line = lax.broadcasted_iota(jnp.int32, (8, block), 0)
        stack = jnp.zeros((8, block), F32)
        for k in range(2):
            mine = part[k : k + 1, :]
            rank = jnp.sum(jnp.where(mine == name, before, 0.0), axis=0, keepdims=True)
            slot = mine * cap + rank.astype(jnp.int32)
            slot_r[k : k + 1, span] = slot
            stack = jnp.where(line == k, slot.astype(F32), stack)
            stack = jnp.where(line == k + 2, gates_t[k : k + 1, span], stack)
        turned = stack.T
        cols[span, :] = turned
        x = tok[span, :].astype(F32)
        centred = x - jnp.mean(x, axis=-1, keepdims=True)
        spread = jnp.mean(centred * centred, axis=-1, keepdims=True)
        d = dmix[span, :].astype(F32)
        tmp[0, span, 0:feats] = (x * lax.rsqrt(spread + 1e-05) * gain[...]).astype(BF16)
        tmp[1, span, 0:feats] = (turned[:, 2:3] * d).astype(BF16)
        tmp[2, span, 0:feats] = (turned[:, 3:4] * d).astype(BF16)
        return carry

    lax.fori_loop(0, rows // block, slots, 0)

    def pack(i, carry):
        e, jj = i // tiles, lax.rem(i, tiles)
        dest = peer(jj)
        want = lax.broadcasted_iota(jnp.int32, (cap, rows), 0) + (dest * per_tile + e) * cap
        first = (slot_r[0:1, :] == want).astype(F32)
        second = (slot_r[1:2, :] == want).astype(F32)
        xs[e, jj] = matmul((first + second).astype(BF16), tmp[0, 0:rows, 0:feats], ((1,), (0,))).astype(BF16)
        ds[e, jj] = (
            matmul(first.astype(BF16), tmp[1, 0:rows, 0:feats], ((1,), (0,)))
            + matmul(second.astype(BF16), tmp[2, 0:rows, 0:feats], ((1,), (0,)))
        ).astype(BF16)

        @pl.when(jj == 0)
        def _():
            for here, there in go_pairs(e, jj, t):
                here().start()

        @pl.when(jj > 0)
        def _():
            for here, there in go_pairs(e, jj, t):
                there().start()

        @pl.when(jnp.logical_and(lax.rem(i, 4) == 3, i // 4 < hops))
        def _():
            ag_event(2 * (i // 4))
            ag_event(2 * (i // 4) + 1)

        return carry

    def ag_event(j):
        e = 2 * (j // (2 * hops)) + lax.rem(j, 2)
        s = lax.rem(j // 2, hops)
        ag_wait(e, s)

        @pl.when(s + 1 < hops)
        def _():
            ag_start(e, s + 1)

        @pl.when(jnp.logical_and(s == hops - 1, e + 2 < per_tile))
        def _():
            ag_start(e + 2, 0)

    lax.fori_loop(0, per_tile * tiles, pack, 0)

    def late(j, carry):
        ag_event(j)
        return carry

    lax.fori_loop(min(2 * hops, 2 * (per_tile * tiles // 4)), 2 * hops, late, 0)
    points = 2 * tiles

    def service_rs(e, k):
        old, young = points // 2 + k // 2, k // 2

        @pl.when(jnp.logical_and(jnp.logical_and(e >= 2, e - 2 < per_tile), jnp.logical_and(lax.rem(k, 2) == 0, old <= last)))
        def _():
            rs_step(e - 2, old)

        @pl.when(jnp.logical_and(jnp.logical_and(e >= 1, e - 1 < per_tile), jnp.logical_and(lax.rem(k, 2) == 1, young <= last)))
        def _():
            rs_step(e - 1, young)

    def service(e, k):
        j = 2 * hops + (e * points + k) // 2

        @pl.when(jnp.logical_and(lax.rem(k, 2) == 0, j < per_tile * hops))
        def _():
            ag_event(j)

        service_rs(e, k)

    def expert(e, carry):
        for jj in range(tiles):
            for here, there in go_pairs(e, jj, source(jj)):
                if jj == 0:
                    here().wait()
                else:
                    there().wait_recv()

        def forward(i, carry):
            span = pl.ds(pl.multiple_of(i * cap, cap), cap)
            x, d = xr[e, i], dr[e, i]
            wide = (feats, hid)
            gate_pre = matmul(x, wgu[e, 0].reshape(wide), ((1,), (0,)))
            up_pre = matmul(x, wgu[e, 1].reshape(wide), ((1,), (0,)))
            d_act = matmul(d, wdn[e].reshape(hid, feats), ((1,), (1,)))
            sigma = jax.nn.sigmoid(gate_pre)
            swish = gate_pre * sigma
            tmp[0, span, :] = (swish * up_pre).astype(BF16)
            tmp[1, span, :] = (d_act * up_pre * sigma * (1.0 + gate_pre * (1.0 - sigma))).astype(BF16)
            tmp[2, span, :] = (d_act * swish).astype(BF16)
            service(e, i)
            return carry

        lax.fori_loop(0, tiles, forward, 0)

        many = tiles * cap
        x_all = xr[e].reshape(many, feats)
        for part in range(2):
            for way in range(2):
                grad = matmul(x_all, tmp[1 + part, 0:many, way * half : (way + 1) * half], ((0,), (0,)))
                ggu[e, way, :, part] = grad.reshape(blks, feats // blks, half).astype(BF16)
        width = min(256, hid)

        def down(i, carry):
            span = pl.ds(pl.multiple_of(i * width, width), width)
            grad = matmul(tmp[0, 0:many, span], dr[e].reshape(many, feats), ((0,), (0,)))
            grad = grad.reshape(width // deep, 2, deep // 2, feats).astype(BF16)
            for c in range(width // deep):
                for way in range(2):
                    gdn[e, way, i * (width // deep) + c] = grad[c, way]
            return carry

        lax.fori_loop(0, hid // width, down, 0)
        rs_start(e, 0)

        def backward(ii, carry):
            jj = lax.rem(ii + 1, tiles)
            i = peer(jj)
            span = pl.ds(pl.multiple_of(i * cap, cap), cap)
            wide = (feats, hid)
            y = matmul(tmp[0, span, :], wdn[e].reshape(hid, feats), ((1,), (0,)))
            d_in = matmul(tmp[1, span, :], wgu[e, 0].reshape(wide), ((1,), (1,)))
            d_in = d_in + matmul(tmp[2, span, :], wgu[e, 1].reshape(wide), ((1,), (1,)))
            xr[e, i] = y.astype(BF16)
            dr[e, i] = d_in.astype(BF16)
            service(e, tiles + ii)

            @pl.when(jj == 0)
            def _():
                for here, there in back_pairs(e, jj, t):
                    here().start()

            @pl.when(jj > 0)
            def _():
                for here, there in back_pairs(e, jj, t):
                    there().start()

            return carry

        lax.fori_loop(0, tiles, backward, 0)
        return carry

    lax.fori_loop(0, per_tile, expert, 0)

    def returned(e, carry):
        for jj in range(tiles):
            for here, there in back_pairs(e, jj, source(jj)):
                if jj == 0:
                    here().wait()
                else:
                    there().wait_recv()
        return carry

    few = min(128, rows)

    def finish(i):
        base = pl.multiple_of(i * few, few)
        span = pl.ds(base, few)
        column = cols[span, :]
        every = experts * cap
        want = lax.broadcasted_iota(jnp.int32, (few, every), 1)
        first = (column[:, 0:1].astype(jnp.int32) == want).astype(F32)
        second = (column[:, 1:2].astype(jnp.int32) == want).astype(F32)
        y = yr[...].reshape(every, feats)
        y0 = matmul(first.astype(BF16), y, ((1,), (0,)))
        y1 = matmul(second.astype(BF16), y, ((1,), (0,)))
        dn = matmul((first + second).astype(BF16), dyr[...].reshape(every, feats), ((1,), (0,)))
        d = dmix[span, :].astype(F32)
        mixed[span, :] = (column[:, 2:3] * y0 + column[:, 3:4] * y1).astype(BF16)
        lane = lax.broadcasted_iota(jnp.int32, (few, 128), 1)
        dots = jnp.where(lane == 0, jnp.sum(d * y0, axis=-1, keepdims=True), 0.0)
        dots = jnp.where(lane == 1, jnp.sum(d * y1, axis=-1, keepdims=True), dots)
        grad_gates[:, span] = dots.T[0:2, :]
        x = tok[span, :].astype(F32)
        centred = x - jnp.mean(x, axis=-1, keepdims=True)
        spread = jnp.mean(centred * centred, axis=-1, keepdims=True)
        r = lax.rsqrt(spread + 1e-05)
        u = dn * gain[...]
        pull = jnp.sum(u * x, axis=-1, keepdims=True) * (r * r * r) / feats
        grad_tok[span, :] = (u * r - pull * centred).astype(BF16)

    begin = points // 2

    def tail(k, carry):
        service_rs(per_tile + k // points, lax.rem(k, points))

        @pl.when(k == begin)
        def _():
            lax.fori_loop(0, per_tile, returned, 0)

        @pl.when(jnp.logical_and(k >= begin, k < begin + rows // few))
        def _():
            finish(k - begin)

        return carry

    lax.fori_loop(0, max(2 * points, begin + rows // few), tail, 0)

    def drain(e, carry):
        def ag_done(s, carry):
            ag_sent(e, s)
            return carry

        lax.fori_loop(0, hops, ag_done, 0)

        def rs_done(s, carry):
            for way in range(2):
                for copy in rs_copies(e, s, way):
                    copy.wait_send()
            return carry

        lax.fori_loop(0, blks - 1, rs_done, 0)
        for jj in range(1, tiles):
            for here, there in go_pairs(e, jj, t) + back_pairs(e, jj, t):
                there().wait_send()
        return carry

    lax.fori_loop(0, per_tile, drain, 0)


def on_device(tiles, blks, tokens, ln_gain, route, gates, w_gate, w_up, w_down, d_mixed):
    rows, feats = tokens.shape
    per_tile, thin, hid = w_gate.shape
    deep = w_down.shape[1]
    experts = per_tile * tiles
    cap = max(2, 3 * rows * route.shape[1] // (2 * experts))
    half = hid // 2
    hops = blks // 2
    vmem = pl.BlockSpec(memory_space=pltpu.VMEM)
    hbm = pl.BlockSpec(memory_space=pl.ANY)
    moved = (per_tile, tiles, cap, feats)
    dma = pltpu.SemaphoreType.DMA
    outs = pl.pallas_call(
        functools.partial(kernel, tiles, blks, per_tile, cap),
        out_shape=(
            jax.ShapeDtypeStruct((rows, feats), BF16),
            jax.ShapeDtypeStruct((2, rows), F32),
            jax.ShapeDtypeStruct((rows, feats), BF16),
            jax.ShapeDtypeStruct((per_tile, thin, hid), F32),
            jax.ShapeDtypeStruct((per_tile, thin, hid), F32),
            jax.ShapeDtypeStruct((per_tile, deep, feats), F32),
        ),
        in_specs=[vmem, vmem, vmem, vmem, hbm, hbm, hbm, vmem],
        out_specs=[vmem] * 6,
        scratch_shapes=[
            pltpu.VMEM((per_tile, 2, blks, thin, hid), BF16),
            pltpu.VMEM((per_tile, blks, deep, feats), BF16),
            pltpu.VMEM(moved, BF16),
            pltpu.VMEM(moved, BF16),
            pltpu.VMEM(moved, BF16),
            pltpu.VMEM(moved, BF16),
            pltpu.VMEM((tiles, per_tile, cap, feats), BF16),
            pltpu.VMEM((tiles, per_tile, cap, feats), BF16),
            pltpu.VMEM((per_tile, 2, blks, 2, thin, half), BF16),
            pltpu.VMEM((per_tile, 2, blks, deep // 2, feats), BF16),
            pltpu.VMEM((per_tile, 2, blks - 1, 2, thin, half), BF16),
            pltpu.VMEM((per_tile, 2, blks - 1, deep // 2, feats), BF16),
            pltpu.VMEM((3, max(rows, tiles * cap), max(hid, feats)), BF16),
            pltpu.VMEM((rows, 8), F32),
            pltpu.VMEM((2, rows), jnp.int32),
            dma((3,)),
            dma((per_tile, 2, hops, 2)),
            dma((per_tile, 2, hops, 2)),
            dma((per_tile, 2, blks - 1, 2)),
            dma((per_tile, 2, blks - 1, 2)),
            dma((per_tile, tiles, 2)),
            dma((per_tile, tiles, 2)),
            dma((per_tile, 2)),
            dma((per_tile, tiles, 2)),
            dma((per_tile, tiles, 2)),
            dma((per_tile, 2)),
        ],
        compiler_params=pltpu.CompilerParams(
            collective_id=0, has_side_effects=True, vmem_limit_bytes=67043328
        ),
    )(tokens, ln_gain.reshape(1, feats), route.T, gates.T, w_gate, w_up, w_down, d_mixed)
    return (outs[0], outs[1].T) + tuple(outs[2:])


def solution(mesh):
    rows_spec = P(("tile", "blk"), None)
    weight_spec = P("tile", "blk", None)
    return jax.shard_map(
        functools.partial(on_device, mesh.shape["tile"], mesh.shape["blk"]),
        mesh=mesh,
        in_specs=(rows_spec, P(), rows_spec, rows_spec) + (weight_spec,) * 3 + (rows_spec,),
        out_specs=(rows_spec,) * 3 + (weight_spec,) * 3,
        check_vma=False,
    )
```

```python
import functools
import math

import jax
import jax.numpy as jnp
from jax import lax
from jax.experimental import pallas as pl
from jax.experimental.pallas import tpu as pltpu
from jax.sharding import PartitionSpec as P

F32 = jnp.float32
BF16 = jnp.bfloat16
MESH = pl.DeviceIdType.MESH


def ring_order(count):
    inner = max(d for d in range(1, math.isqrt(count) + 1) if count % d == 0)
    outer = count // inner
    walk = [row * inner for row in range(outer)]
    for step, row in enumerate(reversed(range(outer))):
        cols = list(range(1, inner))
        if step % 2:
            cols.reverse()
        walk += [row * inner + col for col in cols]
    return walk


def lookup(table, index):
    total = jnp.int32(0)
    for place, value in enumerate(table):
        total = total + jnp.where(index == place, jnp.int32(value), jnp.int32(0))
    return total


def matmul(left, right, dims):
    return lax.dot_general(left, right, (dims, ((), ())), preferred_element_type=F32)


class Later:
    def __init__(self, **parts):
        self.parts = parts

    def __getattr__(self, name):
        return getattr(pltpu.make_async_remote_copy(**self.parts), name)


def kernel(
    tiles, blks, per_tile, cap,
    tok, gain, route_t, gates_t, w_gate, w_up, w_down, dmix,
    mixed, grad_gates, grad_tok, out_gate, out_up, out_dn,
    wgu, wdn, xs, ds, xr, dr, yr, dyr, ggu, gdn, rgu, rdn, tmp, cols, slot_r,
    load_sem, ag_send, ag_recv, rs_send, rs_recv, go_send, go_recv, go_own,
    back_send, back_recv, back_own,
):
    rows, feats = tok.shape
    hid = w_gate.shape[2]
    experts = tiles * per_tile
    half = hid // 2
    deep = hid // blks
    t = lax.axis_index("tile")
    b = lax.axis_index("blk")
    walk = ring_order(blks)
    where_is = [walk.index(i) for i in range(blks)]
    pos = lookup(where_is, b)

    def at(place):
        return lookup(walk, lax.rem(place + 4 * blks, blks))

    ring = (at(pos + 1), at(pos - 1))
    signs = (1, -1)

    def peer(jj):
        return lax.rem(t + jj, tiles)

    def source(jj):
        return lax.rem(t - jj + tiles, tiles)

    loads = []
    for index, (src, dst) in enumerate(
        ((w_gate, wgu.at[:, 0, b]), (w_up, wgu.at[:, 1, b]), (w_down, wdn.at[:, b]))
    ):
        loads.append(pltpu.make_async_copy(src, dst, load_sem.at[index]))
        loads[-1].start()

    barrier = pltpu.get_barrier_semaphore()
    for place in ring:
        pl.semaphore_signal(barrier, inc=1, device_id=(t, place), device_id_type=MESH)
    for jj in range(1, tiles):
        pl.semaphore_signal(barrier, inc=1, device_id=(peer(jj), b), device_id_type=MESH)
    pl.semaphore_wait(barrier, 2 + tiles - 1)
    for load in loads:
        load.wait()

    def ag_copies(e, s, way):
        owner = at(pos - signs[way] * s)
        return [
            pltpu.make_async_remote_copy(
                src_ref=ref, dst_ref=ref,
                send_sem=ag_send.at[e, way, s, part], recv_sem=ag_recv.at[e, way, s, part],
                device_id=(t, ring[way]), device_id_type=MESH,
            )
            for part, ref in enumerate((wgu.at[e, :, owner], wdn.at[e, owner]))
        ]

    def ag_wait_copies(e, s, way):
        owner = at(pos - signs[way] * (s + 1))
        return [
            pltpu.make_async_remote_copy(
                src_ref=ref, dst_ref=ref,
                send_sem=ag_send.at[e, way, s, part], recv_sem=ag_recv.at[e, way, s, part],
                device_id=(t, ring[way]), device_id_type=MESH,
            )
            for part, ref in enumerate((wgu.at[e, :, owner], wdn.at[e, owner]))
        ]

    hops = blks // 2

    def ag_each(e, s, action):
        for way in range(2):
            @pl.when(jnp.logical_or(s < hops - 1, jnp.logical_and(s == hops - 1, lax.rem(e, 2) == way)))
            def _():
                action(e, s, way)

    def ag_start(e, s):
        def go(e, s, way):
            for copy in ag_copies(e, s, way):
                copy.start()
        ag_each(e, s, go)

    def ag_wait(e, s):
        def land(e, s, way):
            for copy in ag_wait_copies(e, s, way):
                copy.wait_recv()
        ag_each(e, s, land)

    def ag_sent(e, s):
        def done(e, s, way):
            for copy in ag_copies(e, s, way):
                copy.wait_send()
        ag_each(e, s, done)

    def rs_copies(e, s, way):
        chunk = at(pos - signs[way] * (s + 1))
        return [
            Later(
                src_ref=src, dst_ref=dst,
                send_sem=rs_send.at[e, way, s, part], recv_sem=rs_recv.at[e, way, s, part],
                device_id=(t, ring[way]), device_id_type=MESH,
            )
            for part, (src, dst) in enumerate((
                (ggu.at[e, way, chunk], rgu.at[e, way, s]),
                (gdn.at[e, way, chunk], rdn.at[e, way, s]),
            ))
        ]

    def rs_start(e, s):
        for way in range(2):
            for copy in rs_copies(e, s, way):
                copy.start()

    last = blks - 2

    def rs_step(e, s):
        for part, (own, landed) in enumerate(((ggu, rgu), (gdn, rdn))):
            for way in range(2):
                rs_copies(e, s, way)[part].wait_recv()
                chunk = at(pos - signs[way] * (s + 2))
                total = own[e, way, chunk].astype(F32) + landed[e, way, s].astype(F32)

                @pl.when(s < last)
                def _():
                    own[e, way, chunk] = total.astype(BF16)
                    rs_copies(e, s + 1, way)[part].start()

                @pl.when(s == last)
                def _():
                    if part:
                        out_dn[e, way * (deep // 2) : (way + 1) * (deep // 2), :] = total
                    else:
                        out_gate[e, :, way * half : (way + 1) * half] = total[0]
                        out_up[e, :, way * half : (way + 1) * half] = total[1]

    def row_copies(src, dst, send, recv, own, e, jj, part, place):
        def here():
            return pltpu.make_async_copy(src, dst, own.at[e, part])

        def there():
            return pltpu.make_async_remote_copy(
                src_ref=src, dst_ref=dst, send_sem=send.at[e, jj, part],
                recv_sem=recv.at[e, jj, part], device_id=(place, b), device_id_type=MESH,
            )

        return here, there

    def go_pairs(e, jj, at_tile):
        return [
            row_copies(src.at[e, jj], dst.at[e, at_tile], go_send, go_recv, go_own, e, jj, part, peer(jj))
            for part, (src, dst) in enumerate(((xs, xr), (ds, dr)))
        ]

    def back_pairs(e, jj, at_tile):
        return [
            row_copies(src.at[e, peer(jj)], dst.at[at_tile, e], back_send, back_recv, back_own, e, jj, part, peer(jj))
            for part, (src, dst) in enumerate(((xr, yr), (dr, dyr)))
        ]

    for e in range(per_tile):
        ag_start(e, 0)

    block = min(256, rows)

    def slots(i, carry):
        base = pl.multiple_of(i * block, block)
        span = pl.ds(base, block)
        names = lax.broadcasted_iota(jnp.int32, (experts, rows), 0)
        count = (route_t[0:1, :] == names).astype(F32) + (route_t[1:2, :] == names).astype(F32)
        row = lax.broadcasted_iota(jnp.int32, (rows, block), 0)
        col = lax.broadcasted_iota(jnp.int32, (rows, block), 1) + base
        before = matmul(count.astype(BF16), (row < col).astype(F32).astype(BF16), ((1,), (0,)))
        part = route_t[:, span]
        name = lax.broadcasted_iota(jnp.int32, (experts, block), 0)
        line = lax.broadcasted_iota(jnp.int32, (8, block), 0)
        stack = jnp.zeros((8, block), F32)
        for k in range(2):
            mine = part[k : k + 1, :]
            rank = jnp.sum(jnp.where(mine == name, before, 0.0), axis=0, keepdims=True)
            slot = mine * cap + rank.astype(jnp.int32)
            slot_r[k : k + 1, span] = slot
            stack = jnp.where(line == k, slot.astype(F32), stack)
            stack = jnp.where(line == k + 2, gates_t[k : k + 1, span], stack)
        turned = stack.T
        cols[span, :] = turned
        x = tok[span, :].astype(F32)
        centred = x - jnp.mean(x, axis=-1, keepdims=True)
        spread = jnp.mean(centred * centred, axis=-1, keepdims=True)
        d = dmix[span, :].astype(F32)
        tmp[0, span, 0:feats] = (x * lax.rsqrt(spread + 1e-05) * gain[...]).astype(BF16)
        tmp[1, span, 0:feats] = (turned[:, 2:3] * d).astype(BF16)
        tmp[2, span, 0:feats] = (turned[:, 3:4] * d).astype(BF16)
        return carry

    lax.fori_loop(0, rows // block, slots, 0)

    def pack(i, carry):
        e, jj = i // tiles, lax.rem(i, tiles)
        dest = peer(jj)
        want = lax.broadcasted_iota(jnp.int32, (cap, rows), 0) + (dest * per_tile + e) * cap
        first = (slot_r[0:1, :] == want).astype(F32)
        second = (slot_r[1:2, :] == want).astype(F32)
        xs[e, jj] = matmul((first + second).astype(BF16), tmp[0, 0:rows, 0:feats], ((1,), (0,))).astype(BF16)
        ds[e, jj] = (
            matmul(first.astype(BF16), tmp[1, 0:rows, 0:feats], ((1,), (0,)))
            + matmul(second.astype(BF16), tmp[2, 0:rows, 0:feats], ((1,), (0,)))
        ).astype(BF16)

        @pl.when(jj == 0)
        def _():
            for here, there in go_pairs(e, jj, t):
                here().start()

        @pl.when(jj > 0)
        def _():
            for here, there in go_pairs(e, jj, t):
                there().start()

        @pl.when(jnp.logical_and(lax.rem(i, 4) == 3, i // 4 < hops))
        def _():
            ag_event(2 * (i // 4))
            ag_event(2 * (i // 4) + 1)

        return carry

    def ag_event(j):
        e = 2 * (j // (2 * hops)) + lax.rem(j, 2)
        s = lax.rem(j // 2, hops)
        ag_wait(e, s)

        @pl.when(s + 1 < hops)
        def _():
            ag_start(e, s + 1)

    lax.fori_loop(0, per_tile * tiles, pack, 0)

    def late(j, carry):
        ag_event(j)
        return carry

    lax.fori_loop(min(2 * hops, 2 * (per_tile * tiles // 4)), 2 * hops, late, 0)
    points = 2 * tiles

    def service_rs(e, k):
        old, young = points // 2 + k // 2, k // 2

        @pl.when(jnp.logical_and(jnp.logical_and(e >= 2, e - 2 < per_tile), jnp.logical_and(lax.rem(k, 2) == 0, old <= last)))
        def _():
            rs_step(e - 2, old)

        @pl.when(jnp.logical_and(jnp.logical_and(e >= 1, e - 1 < per_tile), jnp.logical_and(lax.rem(k, 2) == 1, young <= last)))
        def _():
            rs_step(e - 1, young)

    def service(e, k):
        j = 2 * hops + (e * points + k) // 2

        @pl.when(jnp.logical_and(lax.rem(k, 2) == 0, j < per_tile * hops))
        def _():
            ag_event(j)

        service_rs(e, k)

    def expert(e, carry):
        for jj in range(tiles):
            for here, there in go_pairs(e, jj, source(jj)):
                if jj == 0:
                    here().wait()
                else:
                    there().wait_recv()

        def forward(i, carry):
            span = pl.ds(pl.multiple_of(i * cap, cap), cap)
            x, d = xr[e, i], dr[e, i]
            wide = (feats, hid)
            gate_pre = matmul(x, wgu[e, 0].reshape(wide), ((1,), (0,)))
            up_pre = matmul(x, wgu[e, 1].reshape(wide), ((1,), (0,)))
            d_act = matmul(d, wdn[e].reshape(hid, feats), ((1,), (1,)))
            sigma = jax.nn.sigmoid(gate_pre)
            swish = gate_pre * sigma
            tmp[0, span, :] = (swish * up_pre).astype(BF16)
            tmp[1, span, :] = (d_act * up_pre * sigma * (1.0 + gate_pre * (1.0 - sigma))).astype(BF16)
            tmp[2, span, :] = (d_act * swish).astype(BF16)
            service(e, i)
            return carry

        lax.fori_loop(0, tiles, forward, 0)

        many = tiles * cap
        x_all = xr[e].reshape(many, feats)
        for part in range(2):
            for way in range(2):
                grad = matmul(x_all, tmp[1 + part, 0:many, way * half : (way + 1) * half], ((0,), (0,)))
                ggu[e, way, :, part] = grad.reshape(blks, feats // blks, half).astype(BF16)
        width = min(256, hid)

        def down(i, carry):
            span = pl.ds(pl.multiple_of(i * width, width), width)
            grad = matmul(tmp[0, 0:many, span], dr[e].reshape(many, feats), ((0,), (0,)))
            grad = grad.reshape(width // deep, 2, deep // 2, feats).astype(BF16)
            for c in range(width // deep):
                for way in range(2):
                    gdn[e, way, i * (width // deep) + c] = grad[c, way]
            return carry

        lax.fori_loop(0, hid // width, down, 0)
        rs_start(e, 0)

        def backward(ii, carry):
            jj = lax.rem(ii + 1, tiles)
            i = peer(jj)
            span = pl.ds(pl.multiple_of(i * cap, cap), cap)
            wide = (feats, hid)
            y = matmul(tmp[0, span, :], wdn[e].reshape(hid, feats), ((1,), (0,)))
            d_in = matmul(tmp[1, span, :], wgu[e, 0].reshape(wide), ((1,), (1,)))
            d_in = d_in + matmul(tmp[2, span, :], wgu[e, 1].reshape(wide), ((1,), (1,)))
            xr[e, i] = y.astype(BF16)
            dr[e, i] = d_in.astype(BF16)
            service(e, tiles + ii)

            @pl.when(jj == 0)
            def _():
                for here, there in back_pairs(e, jj, t):
                    here().start()

            @pl.when(jj > 0)
            def _():
                for here, there in back_pairs(e, jj, t):
                    there().start()

            return carry

        lax.fori_loop(0, tiles, backward, 0)
        return carry

    lax.fori_loop(0, per_tile, expert, 0)

    def returned(e, carry):
        for jj in range(tiles):
            for here, there in back_pairs(e, jj, source(jj)):
                if jj == 0:
                    here().wait()
                else:
                    there().wait_recv()
        return carry

    few = min(128, rows)

    def finish(i):
        base = pl.multiple_of(i * few, few)
        span = pl.ds(base, few)
        column = cols[span, :]
        every = experts * cap
        want = lax.broadcasted_iota(jnp.int32, (few, every), 1)
        first = (column[:, 0:1].astype(jnp.int32) == want).astype(F32)
        second = (column[:, 1:2].astype(jnp.int32) == want).astype(F32)
        y = yr[...].reshape(every, feats)
        y0 = matmul(first.astype(BF16), y, ((1,), (0,)))
        y1 = matmul(second.astype(BF16), y, ((1,), (0,)))
        dn = matmul((first + second).astype(BF16), dyr[...].reshape(every, feats), ((1,), (0,)))
        d = dmix[span, :].astype(F32)
        mixed[span, :] = (column[:, 2:3] * y0 + column[:, 3:4] * y1).astype(BF16)
        lane = lax.broadcasted_iota(jnp.int32, (few, 128), 1)
        dots = jnp.where(lane == 0, jnp.sum(d * y0, axis=-1, keepdims=True), 0.0)
        dots = jnp.where(lane == 1, jnp.sum(d * y1, axis=-1, keepdims=True), dots)
        grad_gates[:, span] = dots.T[0:2, :]
        x = tok[span, :].astype(F32)
        centred = x - jnp.mean(x, axis=-1, keepdims=True)
        spread = jnp.mean(centred * centred, axis=-1, keepdims=True)
        r = lax.rsqrt(spread + 1e-05)
        u = dn * gain[...]
        pull = jnp.sum(u * x, axis=-1, keepdims=True) * (r * r * r) / feats
        grad_tok[span, :] = (u * r - pull * centred).astype(BF16)

    begin = points // 2

    def tail(k, carry):
        service_rs(per_tile + k // points, lax.rem(k, points))

        @pl.when(k == begin)
        def _():
            lax.fori_loop(0, per_tile, returned, 0)

        @pl.when(jnp.logical_and(k >= begin, k < begin + rows // few))
        def _():
            finish(k - begin)

        return carry

    lax.fori_loop(0, max(2 * points, begin + rows // few), tail, 0)

    def drain(e, carry):
        def ag_done(s, carry):
            ag_sent(e, s)
            return carry

        lax.fori_loop(0, hops, ag_done, 0)

        def rs_done(s, carry):
            for way in range(2):
                for copy in rs_copies(e, s, way):
                    copy.wait_send()
            return carry

        lax.fori_loop(0, blks - 1, rs_done, 0)
        for jj in range(1, tiles):
            for here, there in go_pairs(e, jj, t) + back_pairs(e, jj, t):
                there().wait_send()
        return carry

    lax.fori_loop(0, per_tile, drain, 0)


def on_device(tiles, blks, tokens, ln_gain, route, gates, w_gate, w_up, w_down, d_mixed):
    rows, feats = tokens.shape
    per_tile, thin, hid = w_gate.shape
    deep = w_down.shape[1]
    experts = per_tile * tiles
    cap = max(2, 3 * rows * route.shape[1] // (2 * experts))
    half = hid // 2
    hops = blks // 2
    vmem = pl.BlockSpec(memory_space=pltpu.VMEM)
    hbm = pl.BlockSpec(memory_space=pl.ANY)
    moved = (per_tile, tiles, cap, feats)
    dma = pltpu.SemaphoreType.DMA
    outs = pl.pallas_call(
        functools.partial(kernel, tiles, blks, per_tile, cap),
        out_shape=(
            jax.ShapeDtypeStruct((rows, feats), BF16),
            jax.ShapeDtypeStruct((2, rows), F32),
            jax.ShapeDtypeStruct((rows, feats), BF16),
            jax.ShapeDtypeStruct((per_tile, thin, hid), F32),
            jax.ShapeDtypeStruct((per_tile, thin, hid), F32),
            jax.ShapeDtypeStruct((per_tile, deep, feats), F32),
        ),
        in_specs=[vmem, vmem, vmem, vmem, hbm, hbm, hbm, vmem],
        out_specs=[vmem] * 6,
        scratch_shapes=[
            pltpu.VMEM((per_tile, 2, blks, thin, hid), BF16),
            pltpu.VMEM((per_tile, blks, deep, feats), BF16),
            pltpu.VMEM(moved, BF16),
            pltpu.VMEM(moved, BF16),
            pltpu.VMEM(moved, BF16),
            pltpu.VMEM(moved, BF16),
            pltpu.VMEM((tiles, per_tile, cap, feats), BF16),
            pltpu.VMEM((tiles, per_tile, cap, feats), BF16),
            pltpu.VMEM((per_tile, 2, blks, 2, thin, half), BF16),
            pltpu.VMEM((per_tile, 2, blks, deep // 2, feats), BF16),
            pltpu.VMEM((per_tile, 2, blks - 1, 2, thin, half), BF16),
            pltpu.VMEM((per_tile, 2, blks - 1, deep // 2, feats), BF16),
            pltpu.VMEM((3, max(rows, tiles * cap), max(hid, feats)), BF16),
            pltpu.VMEM((rows, 8), F32),
            pltpu.VMEM((2, rows), jnp.int32),
            dma((3,)),
            dma((per_tile, 2, hops, 2)),
            dma((per_tile, 2, hops, 2)),
            dma((per_tile, 2, blks - 1, 2)),
            dma((per_tile, 2, blks - 1, 2)),
            dma((per_tile, tiles, 2)),
            dma((per_tile, tiles, 2)),
            dma((per_tile, 2)),
            dma((per_tile, tiles, 2)),
            dma((per_tile, tiles, 2)),
            dma((per_tile, 2)),
        ],
        compiler_params=pltpu.CompilerParams(
            collective_id=0, has_side_effects=True, vmem_limit_bytes=67043328
        ),
    )(tokens, ln_gain.reshape(1, feats), route.T, gates.T, w_gate, w_up, w_down, d_mixed)
    return (outs[0], outs[1].T) + tuple(outs[2:])


def solution(mesh):
    rows_spec = P(("tile", "blk"), None)
    weight_spec = P("tile", "blk", None)
    return jax.shard_map(
        functools.partial(on_device, mesh.shape["tile"], mesh.shape["blk"]),
        mesh=mesh,
        in_specs=(rows_spec, P(), rows_spec, rows_spec) + (weight_spec,) * 3 + (rows_spec,),
        out_specs=(rows_spec,) * 3 + (weight_spec,) * 3,
        check_vma=False,
    )
```
